32 devices in a mesh: group: 2 (over x), inp: 16 (over z, y, core).
Axes of the slice: x: 2, y: 2, z: 4, core: 2. Of those that a mesh axis runs over, the one named last changes fastest.
Arguments:
- raw: bfloat16 [4096, 268288], P(('group', 'inp')), parts along dimension 0, may hold values from -180 to 180
- pfb_taps: float32 [4, 2048], replicated, may hold values from -0.0625 to 0.0625
- flags: int32 [4096], P(('group', 'inp')), parts along dimension 0, may hold values 0 or 1
- chan_table: int32 [8], P('group'), parts along dimension 0, may hold values from 0 to 1023
Outputs:
- visibility: bfloat16 [16384, 2, 2048], P(('group', 'inp')), parts along dimension 0
The draws below stay inside these ranges and needn't reach their ends.
There are 2 independent parts, one for each index of `group`. The reference program is written for one: setup_inputs(seed, part) draws one part's arguments, and reference() takes and returns one part's arrays. A program takes and returns all parts, laid end to end along the dimension named above; an argument that names none is the same for every part. Nothing has to cross between parts.
All inputs are finite; a program needn't handle non-finite values. No bound on the sum of `flags` on one device may be relied on, other than what follows from the above.
Results may differ from the reference program's by a relative error of at most 0.0074.
Values may be sent and summed in bfloat16 or wider, within the bound.
A program may use at most 256 MiB of HBM per device.

```python
import math
import jax
import jax.numpy as jnp
from jax import lax

INPUTS = 2048
FFT_LEN = 2048
CHANNELS = 1024
FILTER_TAPS = 4
SPECTRA = 128
SELECTED = 4


def draw_raw(key, part):
    base_key = jax.random.fold_in(key, 11)
    gain_key = jax.random.fold_in(key, 23)
    frame_count = SPECTRA + FILTER_TAPS - 1
    rise_factor = jnp.exp(math.log(3.0) * jnp.arange(INPUTS, dtype=jnp.float32) / INPUTS)
    spread_factor = jnp.exp(math.log(10.0) * jax.random.uniform(gain_key, (INPUTS,), jnp.float32))
    input_gain = (rise_factor * spread_factor)[:, None, None]
    samples = jnp.clip(jax.random.normal(base_key, (INPUTS, frame_count, FFT_LEN), jnp.float32), -6.0, 6.0)
    return (samples * input_gain).reshape(INPUTS, frame_count * FFT_LEN).astype(jnp.bfloat16)


def with_ends(result, rng, least, largest):
    longest = result.shape.index(max(result.shape))
    spots = []
    for shift in (0, 1):
        where = [jax.random.randint(jax.random.fold_in(rng, axis), (), 0, length) for axis, length in enumerate(result.shape)]
        where[longest] = (where[longest] + shift) % result.shape[longest]
        spots.append(tuple(where))
    return result.at[spots[0]].set(least).at[spots[1]].set(largest)


def gaussian(key, shape, spread, most, kind=jnp.bfloat16):
    result = spread * jax.random.normal(key, shape, jnp.float32)
    return jnp.clip(result, min=-most, max=most).astype(kind)


def setup_inputs(seed: int = 0, part: int = 0) -> dict:
    seeds = jax.random.split(jax.random.key(seed), 5)
    part_splits = jax.random.split(jax.random.fold_in(seeds[4], part), 5)
    raw = draw_raw(jax.random.fold_in(jax.random.fold_in(seeds[4], part), 71), part)
    pfb_taps = gaussian(seeds[1], (FILTER_TAPS, FFT_LEN), (FILTER_TAPS * FFT_LEN) ** -0.5, 0.0625, jnp.float32)
    flags = with_ends((jax.random.randint(part_splits[2], (INPUTS,), 0, 16) < 15).astype(jnp.int32), jax.random.fold_in(part_splits[2], 1), 0, 1)
    chan_table = with_ends(jax.random.randint(part_splits[3], (SELECTED,), 0, CHANNELS), jax.random.fold_in(part_splits[3], 1), 0, CHANNELS - 1).astype(jnp.int32)
    return dict(raw=raw, pfb_taps=pfb_taps, flags=flags, chan_table=chan_table)


def make_basis(chan_table):
    sample_index = jnp.arange(FFT_LEN, dtype=jnp.int32)
    phase_steps = sample_index[:, None] * chan_table[None, :].astype(jnp.int32) % FFT_LEN
    angle = phase_steps.astype(jnp.float32) * (2.0 * math.pi / FFT_LEN)
    return jnp.concatenate([jnp.cos(angle), -jnp.sin(angle)], axis=1).astype(jnp.bfloat16)

def reference(raw, pfb_taps, flags, chan_table):
    basis = make_basis(chan_table).astype(jnp.float32)
    block_rows = 128
    count = SPECTRA
    shaped = raw.reshape(INPUTS // block_rows, block_rows, count + FILTER_TAPS - 1, FFT_LEN)

    def transform(frames):
        filtered = frames[:, 0:count, :].astype(jnp.float32) * pfb_taps[0]
        for tap in range(1, FILTER_TAPS):
            filtered = filtered + frames[:, tap:tap + count, :].astype(jnp.float32) * pfb_taps[tap]
        filtered = filtered.astype(jnp.bfloat16).astype(jnp.float32)
        spectrum = jnp.einsum('itn,nk->ikt', filtered, basis, precision=lax.Precision.HIGHEST, preferred_element_type=jnp.float32)
        squares = lax.optimization_barrier(jnp.mean(jnp.square(frames.astype(jnp.float32)), axis=(1, 2))) + 1e-06
        return (spectrum, squares)
    spectra, power = lax.map(transform, shaped)
    spectra = spectra.reshape(INPUTS, 2 * SELECTED, count)
    power = power.reshape(INPUTS)
    spectra = (spectra * flags.astype(jnp.float32)[:, None, None]).astype(jnp.bfloat16)
    grouped = spectra.reshape(INPUTS, 2, SELECTED, count)
    scales = lax.rsqrt(power)
    per_channel = jnp.transpose(grouped, (2, 0, 1, 3))

    def correlate(channel_data):
        data = channel_data.astype(jnp.float32)
        real_part = data[:, 0, :]
        imag_part = data[:, 1, :]

        def product(left, right):
            return jnp.dot(left, right.T, precision=lax.Precision.HIGHEST, preferred_element_type=jnp.float32)
        real_vis = product(real_part, real_part) + product(imag_part, imag_part)
        imag_vis = product(imag_part, real_part) - product(real_part, imag_part)
        stacked = jnp.stack([real_vis, imag_vis], axis=1)
        scaled = stacked * (1.0 / SPECTRA) * scales[:, None, None] * scales[None, None, :]
        return scaled.astype(jnp.bfloat16)
    return lax.map(correlate, per_channel).reshape(SELECTED * INPUTS, 2, INPUTS)
```

```python
import functools
import math

import jax
import jax.numpy as jnp
from jax import lax
from jax.experimental import pallas as pl
from jax.experimental.pallas import tpu as pltpu
from jax.sharding import PartitionSpec as P

FFT_LEN = 2048
FILTER_TAPS = 4
SPECTRA = 128
ROW_BLOCKS = 4
CHUNK = 8
SLOTS = 3
LANES = 128
MESH = pl.DeviceIdType.MESH


def make_basis(chan_table):
    sample_index = jnp.arange(FFT_LEN, dtype=jnp.int32)
    phase_steps = sample_index[:, None] * chan_table[None, :] % FFT_LEN
    angle = phase_steps.astype(jnp.float32) * (2.0 * math.pi / FFT_LEN)
    return jnp.concatenate([jnp.cos(angle), -jnp.sin(angle)], axis=1).astype(jnp.bfloat16)


def row_product(left, right):
    return lax.dot_general(
        left, right, (((1,), (1,)), ((), ())), preferred_element_type=jnp.float32
    )


def plain_device(raw, pfb_taps, flags, chan_table):
    width = raw.shape[0]
    count = SPECTRA
    frames = raw.reshape(width, count + FILTER_TAPS - 1, FFT_LEN)
    filtered = pfb_taps[0] * frames[:, 0:count, :].astype(jnp.float32)
    for tap in range(1, FILTER_TAPS):
        filtered = filtered + pfb_taps[tap] * frames[:, tap : tap + count, :].astype(jnp.float32)
    filtered = filtered.astype(jnp.bfloat16).reshape(width * count, FFT_LEN)
    basis = make_basis(chan_table)
    selected = chan_table.shape[0]
    plain = jnp.dot(filtered, basis, preferred_element_type=jnp.float32)
    plain = plain.reshape(width, count, 2 * selected) * flags.astype(jnp.float32)[:, None, None]
    spectra = jnp.transpose(plain.astype(jnp.bfloat16), (0, 2, 1))
    grouped = spectra.reshape(width, 2, selected, count)
    squares = lax.dot_general(
        raw, raw, (((1,), (1,)), ((0,), (0,))), preferred_element_type=jnp.float32
    )
    power = squares * (1.0 / raw.shape[1]) + 1e-06
    power_all = lax.all_gather(power, "inp", axis=0, tiled=True)
    outgoing = jnp.repeat(grouped, ROW_BLOCKS, axis=2).reshape(
        width, 2, selected * ROW_BLOCKS * count
    )
    columns = lax.all_to_all(outgoing, "inp", split_axis=2, concat_axis=0, tiled=True)
    block_index = lax.axis_index("inp") % ROW_BLOCKS
    rows_here = columns.shape[0] // ROW_BLOCKS
    depth = columns.shape[2]
    mine = lax.dynamic_slice_in_dim(columns, block_index * rows_here, rows_here, 0)
    flat_columns = columns.reshape(columns.shape[0], 2 * depth)
    real_vis = row_product(mine.reshape(rows_here, 2 * depth), flat_columns)
    imag_vis = row_product(mine[:, 1, :], columns[:, 0, :]) - row_product(
        mine[:, 0, :], columns[:, 1, :]
    )
    scales = lax.rsqrt(power_all)
    my_scales = lax.dynamic_slice_in_dim(scales, block_index * rows_here, rows_here, 0)
    left_scale = my_scales[:, None] * (1.0 / SPECTRA)
    right_scale = scales[None, :]
    real_out = real_vis * left_scale * right_scale
    imag_out = imag_vis * left_scale * right_scale
    return jnp.stack([real_out, imag_out], axis=1).astype(jnp.bfloat16)


def front_kernel(
    n, raw, w_ref, flags_ref, g_out, p_out, buf, zbuf, abuf, cbuf, acc,
    load_sem, s1, r1, s2, r2, sp, rp,
):
    width = flags_ref.shape[0]
    lines = n // ROW_BLOCKS
    group = lax.axis_index("group")
    me = lax.axis_index("inp")
    line, spot = me // ROW_BLOCKS, me % ROW_BLOCKS
    full = SPECTRA // CHUNK
    tail = FILTER_TAPS - 1

    def load(c, slot, j):
        return pltpu.make_async_copy(
            raw.at[:, pl.ds((c * CHUNK + j) * FFT_LEN, FFT_LEN)],
            buf.at[slot, pl.ds(j * width, width), :],
            load_sem.at[slot, j],
        )

    def start(c, slot, frames):
        for j in range(frames):
            load(c, slot, j).start()

    for c in range(SLOTS):
        start(c, c, CHUNK)
    barrier = pltpu.get_barrier_semaphore()
    for step in range(1, n):
        pl.semaphore_signal(
            barrier, inc=1, device_id=(group, lax.rem(me + step, n)), device_id_type=MESH
        )
    acc[...] = jnp.zeros_like(acc)
    zbuf[0 : tail * width, :] = jnp.zeros((tail * width, LANES), jnp.float32)
    lane = lax.broadcasted_iota(jnp.int32, (width, LANES), 1)
    pl.semaphore_wait(barrier, n - 1)

    def process(slot, frames):
        total = acc[...]
        for j in range(frames):
            for k in range(FFT_LEN // LANES):
                x = buf[slot, j * width : (j + 1) * width, k * LANES : (k + 1) * LANES]
                x = x.astype(jnp.float32)
                total = total + x * x
        acc[...] = total
        y = jnp.dot(
            buf[slot, 0 : frames * width, :], w_ref[...], preferred_element_type=jnp.float32
        )
        zbuf[tail * width : (tail + frames) * width, :] = y + pltpu.roll(y, LANES // 2, 1)
        placed = jnp.zeros((width, LANES), jnp.float32)
        for j in range(frames):
            value = None
            for p in range(FILTER_TAPS):
                z = zbuf[(j + p) * width : (j + p + 1) * width, :]
                shift = (j - p) * 8 % LANES
                z = z if shift == 0 else pltpu.roll(z, shift, 1)
                value = z if value is None else value + z
            placed = jnp.where(lane // 8 == j, value, placed)
        return placed

    def first(g, step):
        other = lax.rem(line + step, lines)
        return pltpu.make_async_remote_copy(
            src_ref=cbuf.at[other, g],
            dst_ref=g_out.at[pl.ds(me * width, width), g * LANES : (g + 1) * LANES],
            send_sem=s1.at[g, step - 1],
            recv_sem=r1.at[g, step - 1],
            device_id=(group, other * ROW_BLOCKS + spot),
            device_id_type=MESH,
        )

    def second(g, step, turn):
        source = lax.rem(line - step + lines, lines) * ROW_BLOCKS + spot
        rows = g_out.at[pl.ds(source * width, width), g * LANES : (g + 1) * LANES]
        return pltpu.make_async_remote_copy(
            src_ref=cbuf.at[line, g] if step == 0 else rows,
            dst_ref=rows,
            send_sem=s2.at[g, step, turn - 1],
            recv_sem=r2.at[g, step, turn - 1],
            device_id=(group, line * ROW_BLOCKS + lax.rem(spot + turn, ROW_BLOCKS)),
            device_id_type=MESH,
        )

    def send(g):
        row = lax.broadcasted_iota(jnp.int32, (LANES, LANES), 0)
        col = lax.broadcasted_iota(jnp.int32, (LANES, LANES), 1)
        perm = jnp.where(
            row == (col % 16) * 8 + (col // 16) % 2 * 4 + col // 32, 1.0, 0.0
        ).astype(jnp.bfloat16)
        flag = flags_ref[...]
        columns = [jnp.zeros((width, LANES), jnp.float32)] * lines
        for h in range(4):
            d = (1 + 4 * g + h) % 8
            both = jnp.where(
                lane < LANES // 2, abuf[2 * d], pltpu.roll(abuf[2 * d + 1], LANES // 2, 1)
            )
            spectra = (both * flag).astype(jnp.bfloat16)
            b = jnp.dot(spectra, perm, preferred_element_type=jnp.float32)
            for k in range(lines):
                shift = (h - k) * 32 % LANES
                moved = b if shift == 0 else pltpu.roll(b, shift, 1)
                columns[k] = jnp.where(lane // 32 == h, moved, columns[k])
        for k in range(lines):
            cbuf[k, g] = columns[k].astype(jnp.bfloat16)
        for step in range(1, lines):
            first(g, step).start()
        for turn in range(1, ROW_BLOCKS):
            second(g, 0, turn).start()
        g_out[pl.ds(me * width, width), g * LANES : (g + 1) * LANES] = cbuf[line, g]

    def forward(g):
        for step in range(1, lines):
            first(g, step).wait_recv()
            for turn in range(1, ROW_BLOCKS):
                second(g, step, turn).start()

    def body(c, carry):
        slot = lax.rem(c, SLOTS)
        for j in range(CHUNK):
            load(c, slot, j).wait()
        abuf[c] = process(slot, CHUNK)

        @pl.when(c + SLOTS < full)
        def _():
            start(c + SLOTS, slot, CHUNK)

        @pl.when(c + SLOTS == full)
        def _():
            start(c + SLOTS, slot, tail)

        zbuf[0 : tail * width, :] = zbuf[CHUNK * width : (CHUNK + tail) * width, :]

        @pl.when(c == 9)
        def _():
            send(0)

        @pl.when(c == 13)
        def _():
            forward(0)

        return carry

    lax.fori_loop(0, full, body, 0)
    last = full % SLOTS
    for j in range(tail):
        load(full, last, j).wait()
    placed = process(last, tail)
    abuf[0] = jnp.where(lane < 8 * tail, placed, abuf[0])
    send(1)
    squares = jnp.sum(jnp.transpose(acc[...]), axis=0, keepdims=True)
    power = squares * (1.0 / raw.shape[1]) + 1e-06
    p_out[me] = jnp.broadcast_to(power, p_out.shape[1:])

    def share(step):
        return pltpu.make_async_remote_copy(
            src_ref=p_out.at[me],
            dst_ref=p_out.at[me],
            send_sem=sp.at[step - 1],
            recv_sem=rp.at[step - 1],
            device_id=(group, lax.rem(me + step, n)),
            device_id_type=MESH,
        )

    def shared(step):
        source = lax.rem(me - step + n, n)
        return pltpu.make_async_remote_copy(
            src_ref=p_out.at[source],
            dst_ref=p_out.at[source],
            send_sem=sp.at[step - 1],
            recv_sem=rp.at[step - 1],
            device_id=(group, lax.rem(me + step, n)),
            device_id_type=MESH,
        )

    def landed(g, step, turn):
        source = lax.rem(line - step + lines, lines) * ROW_BLOCKS
        source = source + lax.rem(spot - turn + ROW_BLOCKS, ROW_BLOCKS)
        rows = g_out.at[pl.ds(source * width, width), g * LANES : (g + 1) * LANES]
        return pltpu.make_async_remote_copy(
            src_ref=rows,
            dst_ref=rows,
            send_sem=s2.at[g, step, turn - 1],
            recv_sem=r2.at[g, step, turn - 1],
            device_id=(group, line * ROW_BLOCKS + lax.rem(spot + turn, ROW_BLOCKS)),
            device_id_type=MESH,
        )

    for step in range(1, n):
        share(step).start()
    forward(1)
    for g in range(2):
        for step in range(1, lines):
            first(g, step).wait_send()
        for step in range(lines):
            for turn in range(1, ROW_BLOCKS):
                second(g, step, turn).wait_send()
                landed(g, step, turn).wait_recv()
    for step in range(1, n):
        share(step).wait_send()
        shared(step).wait_recv()


def make_weights(pfb_taps, chan_table):
    basis = make_basis(chan_table).astype(jnp.float32)
    product = pfb_taps.T[:, :, None] * basis[:, None, :]
    product = product.reshape(FFT_LEN, -1)
    high = lax.reduce_precision(product, 8, 7)
    low = product - high
    gap = LANES // 2 - product.shape[1]
    padded = [jnp.pad(part, ((0, 0), (0, gap))) for part in (high, low)]
    return jnp.concatenate(padded, axis=1).astype(jnp.bfloat16)


def fast_device(n, raw, pfb_taps, flags, chan_table):
    width = raw.shape[0]
    lines = n // ROW_BLOCKS
    weights = make_weights(pfb_taps, chan_table)
    vmem = pl.BlockSpec(memory_space=pltpu.VMEM)
    full = SPECTRA // CHUNK
    rows = CHUNK * width
    columns, power_all = pl.pallas_call(
        functools.partial(front_kernel, n),
        out_shape=(
            jax.ShapeDtypeStruct((n * width, 2 * LANES), jnp.bfloat16),
            jax.ShapeDtypeStruct((n, 8, LANES), jnp.float32),
        ),
        in_specs=[pl.BlockSpec(memory_space=pl.ANY), vmem, vmem],
        out_specs=(vmem, vmem),
        scratch_shapes=[
            pltpu.VMEM((SLOTS, rows, FFT_LEN), jnp.bfloat16),
            pltpu.VMEM((rows + (FILTER_TAPS - 1) * width, LANES), jnp.float32),
            pltpu.VMEM((full, width, LANES), jnp.float32),
            pltpu.VMEM((lines, 2, width, LANES), jnp.bfloat16),
            pltpu.VMEM((width, LANES), jnp.float32),
            pltpu.SemaphoreType.DMA((SLOTS, CHUNK)),
            pltpu.SemaphoreType.DMA((2, lines - 1)),
            pltpu.SemaphoreType.DMA((2, lines - 1)),
            pltpu.SemaphoreType.DMA((2, lines, ROW_BLOCKS - 1)),
            pltpu.SemaphoreType.DMA((2, lines, ROW_BLOCKS - 1)),
            pltpu.SemaphoreType.DMA((n - 1,)),
            pltpu.SemaphoreType.DMA((n - 1,)),
        ],
        compiler_params=pltpu.CompilerParams(collective_id=0, has_side_effects=True),
    )(raw, weights, flags.astype(jnp.float32)[:, None])
    return finish(columns, power_all[:, 0, :].reshape(-1))


def finish(columns, power_all):
    total = columns.shape[0]
    rows_here = total // ROW_BLOCKS
    start = lax.axis_index("inp") % ROW_BLOCKS * rows_here
    mine = lax.dynamic_slice_in_dim(columns, start, rows_here, 0)
    halves = mine.reshape(rows_here, 8, 2, 16)
    turned = jnp.stack([halves[:, :, 1], -halves[:, :, 0]], axis=2)
    turned = turned.reshape(rows_here, 2 * LANES)
    real_vis = row_product(mine, columns)
    imag_vis = row_product(turned, columns)
    scales = lax.rsqrt(power_all)
    my_scales = lax.dynamic_slice_in_dim(scales, start, rows_here, 0)
    left_scale = my_scales[:, None] * (1.0 / SPECTRA)
    right_scale = scales[None, :]
    real_out = real_vis * left_scale * right_scale
    imag_out = imag_vis * left_scale * right_scale
    return jnp.stack([real_out, imag_out], axis=1).astype(jnp.bfloat16)


def on_device(n, raw, pfb_taps, flags, chan_table):
    fits = n == ROW_BLOCKS * chan_table.shape[0] and chan_table.shape[0] == 4
    if fits and raw.shape[0] == LANES:
        return fast_device(n, raw, pfb_taps, flags, chan_table)
    return plain_device(raw, pfb_taps, flags, chan_table)


def solution(mesh):
    placed = (P(("group", "inp"), None), P(), P(("group", "inp")), P("group"))
    return jax.shard_map(
        functools.partial(on_device, mesh.shape["inp"]),
        mesh=mesh,
        in_specs=placed,
        out_specs=P(("group", "inp"), None, None),
        check_vma=False,
    )
```
